32 devices in a mesh: depth: 8 (over y, x, core), tile: 4 (over z).
Axes of the slice: x: 2, y: 2, z: 4, core: 2. Of those that a mesh axis runs over, the one named last changes fastest.
Arguments:
- concentration: float32 [64, 128, 256], P('depth', 'tile'), may hold values from -6 to 6
- velocity: float32 [3, 64, 128, 256], P(None, 'depth', 'tile'), may hold values from -6 to 6
- diffusivity: float32 [64, 128, 256], P('depth', 'tile'), may hold values from 0.02 to 0.15
Outputs:
- picture: float32 [4, 128, 256], P(None, 'tile', 'depth')
The draws below stay inside these ranges and needn't reach their ends.
All inputs are finite; a program needn't handle non-finite values.
Results may differ from the reference program's by a relative error of at most 0.0003.
Values sent between devices are 32-bit elements; how exact they have to be, the bound alone decides.
A program may use at most 64 MiB of HBM per device.

```python
import math
import jax
import jax.numpy as jnp
from jax import lax

BX = 32
NY = 256
NZ = 64
NX = 128
N_TILE = 4


def level_of(own_key, extent, pieces, low, high):
    loudness, own = 1.0, jax.random.fold_in(own_key, 6)
    for position, blocks in pieces:
        draws = jnp.exp(jax.random.uniform(jax.random.fold_in(own, position), (blocks,), jnp.float32, low / len(pieces), high / len(pieces)))
        loudness = loudness * jnp.repeat(draws, extent[position] // blocks).reshape([-1 if axis == position else 1 for axis in range(len(extent))])
    return loudness


def noise(key, extent, deviation, reach, shards=(), kind=jnp.bfloat16):
    drawn = jax.random.normal(key, extent, jnp.float32) * deviation
    if len(shards) > 0:
        drawn = level_of(key, extent, shards, -0.22, 0.18) * drawn
    return jnp.clip(drawn, min=-reach, max=reach).astype(kind)


def setup_inputs(seed: int = 0) -> dict:
    seeds = jax.random.split(jax.random.key(seed), 4)
    concentration = noise(seeds[0], (NZ, NX, NY), 1.0, 6.0, ((0, 8), (1, 4)), jnp.float32)
    velocity = noise(seeds[1], (3, NZ, NX, NY), 1.0, 6.0, ((1, 8), (2, 4)), jnp.float32)
    diffusivity = jnp.clip(jnp.exp(math.log(0.15) - 2.014903 * jax.random.uniform(seeds[2], (NZ, NX, NY), jnp.float32) ** level_of(seeds[2], (NZ, NX, NY), ((0, 8), (1, 4)), -0.2, 0.2)), 0.02, 0.15)
    return dict(concentration=concentration, velocity=velocity, diffusivity=diffusivity)


ADVECT = 0.25

def update(padded, velocity, diffusion):
    center = padded[1:-1, 1:-1, 1:-1]
    front_cells = padded[2:, 1:-1, 1:-1]
    back_cells = padded[:-2, 1:-1, 1:-1]
    right_cells = padded[1:-1, 2:, 1:-1]
    left_cells = padded[1:-1, :-2, 1:-1]
    upper_cells = padded[1:-1, 1:-1, 2:]
    lower_cells = padded[1:-1, 1:-1, :-2]
    laplace = front_cells + back_cells + right_cells + left_cells + upper_cells + lower_cells - 6.0 * center
    advect = velocity[0] * (front_cells - back_cells) + velocity[1] * (right_cells - left_cells) + velocity[2] * (upper_cells - lower_cells)
    return center + diffusion * laplace - 0.5 * ADVECT * advect

def emission(mixed_field, bright):
    return jnp.stack([mixed_field, jnp.tanh(mixed_field), mixed_field * mixed_field - 1.0], 0) * bright

def opacity(mixed_field, depth_total):
    return 2.0 / depth_total * (0.5 + jax.nn.sigmoid(2.0 * mixed_field))

def reference(concentration, velocity, diffusivity):
    bright = math.sqrt(NZ)
    padded = jnp.pad(concentration, 1)

    def one_block(block_index):
        offset = (block_index * BX).astype(jnp.int32)
        slab_rows = lax.dynamic_slice_in_dim(padded, offset, BX + 2, 1)
        flow = lax.dynamic_slice_in_dim(velocity, offset, BX, 2)
        spread_rate = lax.dynamic_slice_in_dim(diffusivity, offset, BX, 1)
        mixed_field = update(slab_rows, flow, spread_rate)
        optical = opacity(mixed_field, NZ)
        before = jnp.cumsum(optical, axis=0) - optical
        weight = jnp.exp(-before) * (1.0 - jnp.exp(-optical))
        colors = lax.optimization_barrier(jnp.sum(weight[None] * emission(mixed_field, bright), axis=1))
        coverage = 1.0 - jnp.exp(-lax.optimization_barrier(jnp.sum(optical, axis=0)))
        return jnp.concatenate([colors, coverage[None]], 0)
    blocks = lax.map(one_block, jnp.arange(N_TILE, dtype=jnp.int32))
    return jnp.transpose(blocks, (1, 0, 2, 3)).reshape(4, NX, NY)
```

```python
import functools
import math

import jax
import jax.numpy as jnp
from jax import lax
from jax.experimental import pallas as pl
from jax.experimental.pallas import tpu as pltpu
from jax.sharding import PartitionSpec as P

ADVECT = 0.25
LANES = 128
ROWS = 8
SLOT = LANES // 4


def kernel(
    n,
    tiles,
    conc_hbm,
    vel_hbm,
    diff_hbm,
    out_ref,
    conc,
    vel,
    diff,
    field,
    middle,
    z_before,
    z_after,
    x_edge,
    x_before,
    x_after,
    send,
    recv,
    load_sem,
    halo_send,
    halo_recv,
    part_send,
    part_recv,
):
    layers, width, rays = diff.shape
    groups = width // ROWS
    own = rays // n
    total = layers * n
    half = 0.5 * ADVECT
    bright = math.sqrt(total)
    me = lax.axis_index("depth")
    lane_block = lax.axis_index("tile")
    first, last = me == 0, me == n - 1
    left, right = lane_block == 0, lane_block == tiles - 1

    load_conc = pltpu.make_async_copy(
        conc_hbm, conc.at[:, pl.ds(ROWS, width), :], load_sem.at[0]
    )
    load_conc.start()
    barrier = pltpu.get_barrier_semaphore()
    for k in range(1, n):
        pl.semaphore_signal(
            barrier,
            inc=1,
            device_id={"depth": lax.rem(me + k, n)},
            device_id_type=pl.DeviceIdType.MESH,
        )

    @pl.when(jnp.logical_not(left))
    def _():
        pl.semaphore_signal(
            barrier,
            inc=1,
            device_id={"tile": lane_block - 1},
            device_id_type=pl.DeviceIdType.MESH,
        )

    @pl.when(jnp.logical_not(right))
    def _():
        pl.semaphore_signal(
            barrier,
            inc=1,
            device_id={"tile": lane_block + 1},
            device_id_type=pl.DeviceIdType.MESH,
        )

    load_vel = pltpu.make_async_copy(vel_hbm, vel, load_sem.at[1])
    load_vel.start()
    load_diff = pltpu.make_async_copy(diff_hbm, diff, load_sem.at[2])
    load_diff.start()

    zero_rows = jnp.zeros((ROWS, rays), jnp.float32)
    for z in range(layers):
        conc[z, pl.ds(0, ROWS), :] = zero_rows
        conc[z, pl.ds(ROWS + width, ROWS), :] = zero_rows

    @pl.when(first)
    def _():
        z_before[...] = jnp.zeros_like(z_before)

    @pl.when(last)
    def _():
        z_after[...] = jnp.zeros_like(z_after)

    @pl.when(left)
    def _():
        x_before[...] = jnp.zeros_like(x_before)

    @pl.when(right)
    def _():
        x_after[...] = jnp.zeros_like(x_after)

    load_conc.wait()
    for z in range(layers):
        x_edge[0, pl.ds(z, 1), :] = conc[z, pl.ds(ROWS, 1), :]
        x_edge[1, pl.ds(z, 1), :] = conc[z, pl.ds(ROWS + width - 1, 1), :]

    def halo(index, source, target, device):
        return pltpu.make_async_remote_copy(
            src_ref=source,
            dst_ref=target,
            send_sem=halo_send.at[index],
            recv_sem=halo_recv.at[index],
            device_id=device,
            device_id_type=pl.DeviceIdType.MESH,
        )

    inner = pl.ds(ROWS, width)
    deeper = halo(0, conc.at[layers - 1, inner], z_before, {"depth": lax.rem(me + 1, n)})
    nearer = halo(1, conc.at[0, inner], z_after, {"depth": lax.rem(me + n - 1, n)})
    rightward = halo(2, x_edge.at[1], x_before, {"tile": lax.rem(lane_block + 1, tiles)})
    leftward = halo(3, x_edge.at[0], x_after, {"tile": lax.rem(lane_block + tiles - 1, tiles)})

    beside = jnp.where(left, 0, 1) + jnp.where(right, 0, 1)
    pl.semaphore_wait(barrier, n - 1 + beside)

    @pl.when(jnp.logical_not(last))
    def _():
        deeper.start()

    @pl.when(jnp.logical_not(first))
    def _():
        nearer.start()

    @pl.when(jnp.logical_not(right))
    def _():
        rightward.start()

    @pl.when(jnp.logical_not(left))
    def _():
        leftward.start()

    load_vel.wait()
    load_diff.wait()

    lane = lax.broadcasted_iota(jnp.int32, (ROWS, rays), 1)
    row = lax.broadcasted_iota(jnp.int32, (ROWS, rays), 0)

    def local_update(z, start):
        rows = pl.ds(start, ROWS)
        here = conc[z, pl.ds(ROWS + start, ROWS), :]
        left_cells = conc[z, pl.ds(ROWS + start - 1, ROWS), :]
        right_cells = conc[z, pl.ds(ROWS + start + 1, ROWS), :]
        lower_cells = jnp.where(lane == 0, 0.0, pltpu.roll(here, 1, 1))
        upper_cells = jnp.where(lane == rays - 1, 0.0, pltpu.roll(here, rays - 1, 1))
        spread = left_cells + right_cells + lower_cells + upper_cells
        flow = vel[1, z, rows, :] * (right_cells - left_cells) + vel[2, z, rows, :] * (
            upper_cells - lower_cells
        )
        if z > 0:
            back = conc[z - 1, pl.ds(ROWS + start, ROWS), :]
            spread = spread + back
        if z < layers - 1:
            front = conc[z + 1, pl.ds(ROWS + start, ROWS), :]
            spread = spread + front
        if 0 < z < layers - 1:
            slope = front - back
        elif z > 0:
            slope = -back
        else:
            slope = front
        flow = flow + vel[0, z, rows, :] * slope
        return here + diff[z, rows, :] * (spread - 6.0 * here) - half * flow

    def shade(mixed):
        bend = jnp.tanh(mixed)
        passed = jnp.exp((bend + 2.0) * (-1.0 / total))
        return bend, passed

    def add_cell(state, mixed):
        bend, passed = shade(mixed)
        if state is None:
            weight = 1.0 - passed
            return weight * mixed, weight * bend, weight * (mixed * mixed - 1.0), passed
        one, two, three, through = state
        weight = through * (1.0 - passed)
        return (
            one + weight * mixed,
            two + weight * bend,
            three + weight * (mixed * mixed - 1.0),
            through * passed,
        )

    order = list(range(1, groups - 1)) + [0, groups - 1]
    for g in order:
        start = g * ROWS
        edge = g in (0, groups - 1)
        state = None
        for z in range(layers):
            mixed = local_update(z, start)
            if edge or z in (0, layers - 1):
                field[z, pl.ds(start, ROWS), :] = mixed
            else:
                state = add_cell(state, mixed)
        if not edge:
            for c in range(4):
                middle[c, pl.ds(start, ROWS), :] = state[c]

    @pl.when(jnp.logical_not(first))
    def _():
        deeper.wait_recv()

    @pl.when(jnp.logical_not(last))
    def _():
        nearer.wait_recv()

    slot_of = lax.broadcasted_iota(jnp.int32, (ROWS, LANES), 1) // SLOT

    def pack(state, d):
        tile, offset = divmod(d * own, LANES)
        block = None
        for c in range(4):
            piece = state[c][:, tile * LANES : (tile + 1) * LANES]
            shift = (SLOT * c - offset) % LANES
            if shift:
                piece = pltpu.roll(piece, shift, 1)
            block = piece if block is None else jnp.where(slot_of == c, piece, block)
        return block

    def part(g, k):
        target = lax.rem(me + k, n)
        return pltpu.make_async_remote_copy(
            src_ref=send.at[g, target],
            dst_ref=recv.at[g, me],
            send_sem=part_send.at[g, k],
            recv_sem=part_recv.at[g, k],
            device_id={"depth": target},
            device_id_type=pl.DeviceIdType.MESH,
        )

    def corrected(z, start):
        rows = pl.ds(start, ROWS)
        mixed = field[z, rows, :]
        spread = diff[z, rows, :]
        if z == 0:
            mixed = mixed + z_before[rows, :] * (spread + half * vel[0, z, rows, :])
        if z == layers - 1:
            mixed = mixed + z_after[rows, :] * (spread - half * vel[0, z, rows, :])
        if start == 0:
            beside = jnp.where(row == 0, x_before[pl.ds(z, 1), :], 0.0)
            mixed = mixed + beside * (spread + half * vel[1, z, rows, :])
        if start == width - ROWS:
            beside = jnp.where(row == ROWS - 1, x_after[pl.ds(z, 1), :], 0.0)
            mixed = mixed + beside * (spread - half * vel[1, z, rows, :])
        return mixed

    waited = False
    for g in order:
        start = g * ROWS
        edge = g in (0, groups - 1)
        if edge and not waited:
            waited = True

            @pl.when(jnp.logical_not(left))
            def _():
                rightward.wait_recv()

            @pl.when(jnp.logical_not(right))
            def _():
                leftward.wait_recv()

        state = add_cell(None, corrected(0, start))
        if edge:
            for z in range(1, layers):
                state = add_cell(state, corrected(z, start))
        else:
            rows = pl.ds(start, ROWS)
            through = state[3]
            state = tuple(state[c] + through * middle[c, rows, :] for c in range(3)) + (
                through * middle[3, rows, :],
            )
            state = add_cell(state, corrected(layers - 1, start))
        state = tuple(bright * state[c] for c in range(3)) + (state[3],)
        for d in range(n):
            send[g, d] = pack(state, d)
        for k in range(n - 1, 0, -1):
            part(g, k).start()

    for g in order:
        recv[g, me] = send[g, me]

    for g in order:
        for k in range(1, n):
            part(g, k).wait_recv()
        through = None
        for s in range(n):
            block = recv[g, s]
            passed = jnp.where(slot_of >= 2, block, pltpu.roll(block, LANES // 2, 1))
            passed = jnp.where(slot_of % 2 == 1, passed, pltpu.roll(passed, LANES - SLOT, 1))
            if through is None:
                picture, through = block, passed
            else:
                picture, through = picture + through * block, through * passed
        rows = pl.ds(g * ROWS, ROWS)
        for c in range(3):
            color = pltpu.roll(picture, LANES - SLOT * c, 1) if c else picture
            out_ref[c, rows, :] = color[:, :own]
        out_ref[3, rows, :] = (1.0 - through)[:, :own]

    @pl.when(jnp.logical_not(last))
    def _():
        deeper.wait_send()

    @pl.when(jnp.logical_not(first))
    def _():
        nearer.wait_send()

    @pl.when(jnp.logical_not(right))
    def _():
        rightward.wait_send()

    @pl.when(jnp.logical_not(left))
    def _():
        leftward.wait_send()

    for g in order:
        for k in range(1, n):
            part(g, k).wait_send()


def solution(mesh):
    n, tiles = mesh.shape["depth"], mesh.shape["tile"]

    def body(concentration, velocity, diffusivity):
        layers, width, rays = concentration.shape
        groups = width // ROWS
        own = rays // n
        assert own <= SLOT and LANES % own == 0
        scratch = [
            pltpu.VMEM((layers, width + 2 * ROWS, rays), jnp.float32),
            pltpu.VMEM(velocity.shape, jnp.float32),
            pltpu.VMEM(diffusivity.shape, jnp.float32),
            pltpu.VMEM((layers, width, rays), jnp.float32),
            pltpu.VMEM((4, width, rays), jnp.float32),
            pltpu.VMEM((width, rays), jnp.float32),
            pltpu.VMEM((width, rays), jnp.float32),
            pltpu.VMEM((2, layers, rays), jnp.float32),
            pltpu.VMEM((layers, rays), jnp.float32),
            pltpu.VMEM((layers, rays), jnp.float32),
            pltpu.VMEM((groups, n, ROWS, LANES), jnp.float32),
            pltpu.VMEM((groups, n, ROWS, LANES), jnp.float32),
            pltpu.SemaphoreType.DMA((3,)),
            pltpu.SemaphoreType.DMA((4,)),
            pltpu.SemaphoreType.DMA((4,)),
            pltpu.SemaphoreType.DMA((groups, n)),
            pltpu.SemaphoreType.DMA((groups, n)),
        ]
        return pl.pallas_call(
            functools.partial(kernel, n, tiles),
            out_shape=jax.ShapeDtypeStruct((4, width, own), jnp.float32),
            in_specs=[pl.BlockSpec(memory_space=pl.ANY)] * 3,
            out_specs=pl.BlockSpec(memory_space=pltpu.VMEM),
            scratch_shapes=scratch,
            compiler_params=pltpu.CompilerParams(collective_id=0, has_side_effects=True),
        )(concentration, velocity, diffusivity)

    return jax.shard_map(
        body,
        mesh=mesh,
        in_specs=(
            P("depth", "tile", None),
            P(None, "depth", "tile", None),
            P("depth", "tile", None),
        ),
        out_specs=P(None, "tile", "depth"),
        check_vma=False,
    )
```

```python
import functools
import math

import jax
import jax.numpy as jnp
from jax import lax
from jax.experimental import pallas as pl
from jax.experimental.pallas import tpu as pltpu
from jax.sharding import PartitionSpec as P

ADVECT = 0.25
LANES = 128
ROWS = 8
SLOT = LANES // 4


def kernel(
    n,
    tiles,
    conc_hbm,
    vel_hbm,
    diff_hbm,
    out_ref,
    conc,
    vel,
    diff,
    field,
    middle,
    z_before,
    z_after,
    x_edge,
    x_before,
    x_after,
    send,
    recv,
    load_sem,
    halo_send,
    halo_recv,
    part_send,
    part_recv,
):
    layers, width, rays = diff.shape
    groups = width // ROWS
    own = rays // n
    total = layers * n
    half = 0.5 * ADVECT
    bright = math.sqrt(total)
    me = lax.axis_index("depth")
    lane_block = lax.axis_index("tile")
    first, last = me == 0, me == n - 1
    left, right = lane_block == 0, lane_block == tiles - 1

    load_conc = pltpu.make_async_copy(
        conc_hbm, conc.at[:, pl.ds(ROWS, width), :], load_sem.at[0]
    )
    load_conc.start()
    barrier = pltpu.get_barrier_semaphore()
    for k in range(1, n):
        pl.semaphore_signal(
            barrier,
            inc=1,
            device_id={"depth": lax.rem(me + k, n)},
            device_id_type=pl.DeviceIdType.MESH,
        )

    @pl.when(jnp.logical_not(left))
    def _():
        pl.semaphore_signal(
            barrier,
            inc=1,
            device_id={"tile": lane_block - 1},
            device_id_type=pl.DeviceIdType.MESH,
        )

    @pl.when(jnp.logical_not(right))
    def _():
        pl.semaphore_signal(
            barrier,
            inc=1,
            device_id={"tile": lane_block + 1},
            device_id_type=pl.DeviceIdType.MESH,
        )

    load_vel = pltpu.make_async_copy(vel_hbm, vel, load_sem.at[1])
    load_vel.start()
    load_diff = pltpu.make_async_copy(diff_hbm, diff, load_sem.at[2])
    load_diff.start()

    zero_rows = jnp.zeros((ROWS, rays), jnp.float32)
    for z in range(layers):
        conc[z, pl.ds(0, ROWS), :] = zero_rows
        conc[z, pl.ds(ROWS + width, ROWS), :] = zero_rows

    @pl.when(first)
    def _():
        z_before[...] = jnp.zeros_like(z_before)

    @pl.when(last)
    def _():
        z_after[...] = jnp.zeros_like(z_after)

    @pl.when(left)
    def _():
        x_before[...] = jnp.zeros_like(x_before)

    @pl.when(right)
    def _():
        x_after[...] = jnp.zeros_like(x_after)

    load_conc.wait()
    for z in range(layers):
        x_edge[0, pl.ds(z, 1), :] = conc[z, pl.ds(ROWS, 1), :]
        x_edge[1, pl.ds(z, 1), :] = conc[z, pl.ds(ROWS + width - 1, 1), :]

    def halo(index, source, target, device):
        return pltpu.make_async_remote_copy(
            src_ref=source,
            dst_ref=target,
            send_sem=halo_send.at[index],
            recv_sem=halo_recv.at[index],
            device_id=device,
            device_id_type=pl.DeviceIdType.MESH,
        )

    inner = pl.ds(ROWS, width)
    deeper = halo(0, conc.at[layers - 1, inner], z_before, {"depth": lax.rem(me + 1, n)})
    nearer = halo(1, conc.at[0, inner], z_after, {"depth": lax.rem(me + n - 1, n)})
    rightward = halo(2, x_edge.at[1], x_before, {"tile": lax.rem(lane_block + 1, tiles)})
    leftward = halo(3, x_edge.at[0], x_after, {"tile": lax.rem(lane_block + tiles - 1, tiles)})

    beside = jnp.where(left, 0, 1) + jnp.where(right, 0, 1)
    pl.semaphore_wait(barrier, n - 1 + beside)

    @pl.when(jnp.logical_not(last))
    def _():
        deeper.start()

    @pl.when(jnp.logical_not(first))
    def _():
        nearer.start()

    @pl.when(jnp.logical_not(right))
    def _():
        rightward.start()

    @pl.when(jnp.logical_not(left))
    def _():
        leftward.start()

    load_vel.wait()
    load_diff.wait()

    lane = lax.broadcasted_iota(jnp.int32, (ROWS, rays), 1)
    row = lax.broadcasted_iota(jnp.int32, (ROWS, rays), 0)

    def local_update(z, start):
        rows = pl.ds(start, ROWS)
        here = conc[z, pl.ds(ROWS + start, ROWS), :]
        left_cells = conc[z, pl.ds(ROWS + start - 1, ROWS), :]
        right_cells = conc[z, pl.ds(ROWS + start + 1, ROWS), :]
        lower_cells = jnp.where(lane == 0, 0.0, pltpu.roll(here, 1, 1))
        upper_cells = jnp.where(lane == rays - 1, 0.0, pltpu.roll(here, rays - 1, 1))
        spread = left_cells + right_cells + lower_cells + upper_cells
        flow = vel[1, z, rows, :] * (right_cells - left_cells) + vel[2, z, rows, :] * (
            upper_cells - lower_cells
        )
        if z > 0:
            back = conc[z - 1, pl.ds(ROWS + start, ROWS), :]
            spread = spread + back
        if z < layers - 1:
            front = conc[z + 1, pl.ds(ROWS + start, ROWS), :]
            spread = spread + front
        if 0 < z < layers - 1:
            slope = front - back
        elif z > 0:
            slope = -back
        else:
            slope = front
        flow = flow + vel[0, z, rows, :] * slope
        return here + diff[z, rows, :] * (spread - 6.0 * here) - half * flow

    def shade(mixed):
        bend = jnp.tanh(mixed)
        passed = jnp.exp((bend + 2.0) * (-1.0 / total))
        return bend, passed

    def add_cell(state, mixed):
        bend, passed = shade(mixed)
        if state is None:
            weight = 1.0 - passed
            return weight * mixed, weight * bend, weight * (mixed * mixed - 1.0), passed
        one, two, three, through = state
        weight = through * (1.0 - passed)
        return (
            one + weight * mixed,
            two + weight * bend,
            three + weight * (mixed * mixed - 1.0),
            through * passed,
        )

    order = list(range(1, groups - 1)) + [0, groups - 1]
    for g in order:
        start = g * ROWS
        edge = g in (0, groups - 1)
        state = None
        for z in range(layers):
            mixed = local_update(z, start)
            if edge or z in (0, layers - 1):
                field[z, pl.ds(start, ROWS), :] = mixed
            else:
                state = add_cell(state, mixed)
        if not edge:
            for c in range(4):
                middle[c, pl.ds(start, ROWS), :] = state[c]

    @pl.when(jnp.logical_not(first))
    def _():
        deeper.wait_recv()

    @pl.when(jnp.logical_not(last))
    def _():
        nearer.wait_recv()

    slot_of = lax.broadcasted_iota(jnp.int32, (ROWS, LANES), 1) // SLOT

    def pack(state, d):
        tile, offset = divmod(d * own, LANES)
        block = None
        for c in range(4):
            piece = state[c][:, tile * LANES : (tile + 1) * LANES]
            shift = (SLOT * c - offset) % LANES
            if shift:
                piece = pltpu.roll(piece, shift, 1)
            block = piece if block is None else jnp.where(slot_of == c, piece, block)
        return block

    def part(g, k):
        target = lax.rem(me + k, n)
        return pltpu.make_async_remote_copy(
            src_ref=send.at[g, target],
            dst_ref=recv.at[g, me],
            send_sem=part_send.at[g, k],
            recv_sem=part_recv.at[g, k],
            device_id={"depth": target},
            device_id_type=pl.DeviceIdType.MESH,
        )

    def corrected(z, start):
        rows = pl.ds(start, ROWS)
        mixed = field[z, rows, :]
        spread = diff[z, rows, :]
        if z == 0:
            mixed = mixed + z_before[rows, :] * (spread + half * vel[0, z, rows, :])
        if z == layers - 1:
            mixed = mixed + z_after[rows, :] * (spread - half * vel[0, z, rows, :])
        if start == 0:
            beside = jnp.where(row == 0, x_before[pl.ds(z, 1), :], 0.0)
            mixed = mixed + beside * (spread + half * vel[1, z, rows, :])
        if start == width - ROWS:
            beside = jnp.where(row == ROWS - 1, x_after[pl.ds(z, 1), :], 0.0)
            mixed = mixed + beside * (spread - half * vel[1, z, rows, :])
        return mixed

    waited = False
    for g in order:
        start = g * ROWS
        edge = g in (0, groups - 1)
        if edge and not waited:
            waited = True

            @pl.when(jnp.logical_not(left))
            def _():
                rightward.wait_recv()

            @pl.when(jnp.logical_not(right))
            def _():
                leftward.wait_recv()

        state = add_cell(None, corrected(0, start))
        if edge:
            for z in range(1, layers):
                state = add_cell(state, corrected(z, start))
        else:
            rows = pl.ds(start, ROWS)
            through = state[3]
            state = tuple(state[c] + through * middle[c, rows, :] for c in range(3)) + (
                through * middle[3, rows, :],
            )
            state = add_cell(state, corrected(layers - 1, start))
        state = tuple(bright * state[c] for c in range(3)) + (state[3],)
        for d in range(n):
            send[g, d] = pack(state, d)
        for k in range(n - 1, 0, -1):
            part(g, k).start()

    for g in order:
        recv[g, me] = send[g, me]

    for g in order:
        for k in range(1, n):
            part(g, k).wait_recv()
        through = None
        for s in range(n):
            block = recv[g, s]
            passed = jnp.where(slot_of >= 2, block, pltpu.roll(block, LANES // 2, 1))
            passed = jnp.where(slot_of % 2 == 1, passed, pltpu.roll(passed, LANES - SLOT, 1))
            if through is None:
                picture, through = block, passed
            else:
                picture, through = picture + through * block, through * passed
        rows = pl.ds(g * ROWS, ROWS)
        for c in range(3):
            color = pltpu.roll(picture, LANES - SLOT * c, 1) if c else picture
            out_ref[c, rows, :] = color[:, :own]
        out_ref[3, rows, :] = (1.0 - through)[:, :own]

    @pl.when(jnp.logical_not(last))
    def _():
        deeper.wait_send()

    @pl.when(jnp.logical_not(first))
    def _():
        nearer.wait_send()

    @pl.when(jnp.logical_not(right))
    def _():
        rightward.wait_send()

    @pl.when(jnp.logical_not(left))
    def _():
        leftward.wait_send()

    for g in order:
        for k in range(1, n):
            part(g, k).wait_send()


def solution(mesh):
    n, tiles = mesh.shape["depth"], mesh.shape["tile"]

    def body(concentration, velocity, diffusivity):
        layers, width, rays = concentration.shape
        groups = width // ROWS
        own = rays // n
        assert own <= SLOT and LANES % own == 0
        scratch = [
            pltpu.VMEM((layers, width + 2 * ROWS, rays), jnp.float32),
            pltpu.VMEM(velocity.shape, jnp.float32),
            pltpu.VMEM(diffusivity.shape, jnp.float32),
            pltpu.VMEM((layers, width, rays), jnp.float32),
            pltpu.VMEM((4, width, rays), jnp.float32),
            pltpu.VMEM((width, rays), jnp.float32),
            pltpu.VMEM((width, rays), jnp.float32),
            pltpu.VMEM((2, layers, rays), jnp.float32),
            pltpu.VMEM((layers, rays), jnp.float32),
            pltpu.VMEM((layers, rays), jnp.float32),
            pltpu.VMEM((groups, n, ROWS, LANES), jnp.float32),
            pltpu.VMEM((groups, n, ROWS, LANES), jnp.float32),
            pltpu.SemaphoreType.DMA((3,)),
            pltpu.SemaphoreType.DMA((4,)),
            pltpu.SemaphoreType.DMA((4,)),
            pltpu.SemaphoreType.DMA((groups, n)),
            pltpu.SemaphoreType.DMA((groups, n)),
        ]
        return pl.pallas_call(
            functools.partial(kernel, n, tiles),
            out_shape=jax.ShapeDtypeStruct((4, width, own), jnp.float32),
            in_specs=[pl.BlockSpec(memory_space=pl.ANY)] * 3,
            out_specs=pl.BlockSpec(memory_space=pltpu.VMEM),
            scratch_shapes=scratch,
            compiler_params=pltpu.CompilerParams(collective_id=0, has_side_effects=True, vmem_limit_bytes=16 << 20),
        )(*[pltpu.with_memory_space_constraint(v, pltpu.HBM) for v in (concentration, velocity, diffusivity)])

    return jax.shard_map(
        body,
        mesh=mesh,
        in_specs=(
            P("depth", "tile", None),
            P(None, "depth", "tile", None),
            P("depth", "tile", None),
        ),
        out_specs=P(None, "tile", "depth"),
        check_vma=False,
    )
```

```python
import functools
import math

import jax
import jax.numpy as jnp
from jax import lax
from jax.experimental import pallas as pl
from jax.experimental.pallas import tpu as pltpu
from jax.sharding import PartitionSpec as P

ADVECT = 0.25
LANES = 128
ROWS = 8
SLOT = LANES // 4


def kernel(
    n,
    tiles,
    conc_hbm,
    vel_hbm,
    diff_hbm,
    out_ref,
    conc,
    vel,
    diff,
    field,
    middle,
    z_before,
    z_after,
    x_edge,
    x_before,
    x_after,
    send,
    recv,
    load_sem,
    halo_send,
    halo_recv,
    part_send,
    part_recv,
):
    layers, width, rays = diff.shape
    groups = width // ROWS
    own = rays // n
    total = layers * n
    half = 0.5 * ADVECT
    bright = math.sqrt(total)
    me = lax.axis_index("depth")
    lane_block = lax.axis_index("tile")
    first, last = me == 0, me == n - 1
    left, right = lane_block == 0, lane_block == tiles - 1

    load_conc = pltpu.make_async_copy(
        conc_hbm, conc.at[:, pl.ds(ROWS, width), :], load_sem.at[0]
    )
    load_conc.start()
    barrier = pltpu.get_barrier_semaphore()
    for k in range(1, n):
        pl.semaphore_signal(
            barrier,
            inc=1,
            device_id={"depth": lax.rem(me + k, n)},
            device_id_type=pl.DeviceIdType.MESH,
        )

    @pl.when(jnp.logical_not(left))
    def _():
        pl.semaphore_signal(
            barrier,
            inc=1,
            device_id={"tile": lane_block - 1},
            device_id_type=pl.DeviceIdType.MESH,
        )

    @pl.when(jnp.logical_not(right))
    def _():
        pl.semaphore_signal(
            barrier,
            inc=1,
            device_id={"tile": lane_block + 1},
            device_id_type=pl.DeviceIdType.MESH,
        )

    load_vel = pltpu.make_async_copy(vel_hbm, vel, load_sem.at[1])
    load_vel.start()
    load_diff = pltpu.make_async_copy(diff_hbm, diff, load_sem.at[2])
    load_diff.start()

    zero_rows = jnp.zeros((ROWS, rays), jnp.float32)
    for z in range(layers):
        conc[z, pl.ds(0, ROWS), :] = zero_rows
        conc[z, pl.ds(ROWS + width, ROWS), :] = zero_rows

    @pl.when(first)
    def _():
        z_before[...] = jnp.zeros_like(z_before)

    @pl.when(last)
    def _():
        z_after[...] = jnp.zeros_like(z_after)

    @pl.when(left)
    def _():
        x_before[...] = jnp.zeros_like(x_before)

    @pl.when(right)
    def _():
        x_after[...] = jnp.zeros_like(x_after)

    load_conc.wait()
    for z in range(layers):
        x_edge[0, pl.ds(z, 1), :] = conc[z, pl.ds(ROWS, 1), :]
        x_edge[1, pl.ds(z, 1), :] = conc[z, pl.ds(ROWS + width - 1, 1), :]

    def halo(index, source, target, device):
        return pltpu.make_async_remote_copy(
            src_ref=source,
            dst_ref=target,
            send_sem=halo_send.at[index],
            recv_sem=halo_recv.at[index],
            device_id=device,
            device_id_type=pl.DeviceIdType.MESH,
        )

    inner = pl.ds(ROWS, width)
    deeper = halo(0, conc.at[layers - 1, inner], z_before, {"depth": lax.rem(me + 1, n)})
    nearer = halo(1, conc.at[0, inner], z_after, {"depth": lax.rem(me + n - 1, n)})
    rightward = halo(2, x_edge.at[1], x_before, {"tile": lax.rem(lane_block + 1, tiles)})
    leftward = halo(3, x_edge.at[0], x_after, {"tile": lax.rem(lane_block + tiles - 1, tiles)})

    beside = jnp.where(left, 0, 1) + jnp.where(right, 0, 1)
    pl.semaphore_wait(barrier, n - 1 + beside)

    @pl.when(jnp.logical_not(right))
    def _():
        rightward.start()

    @pl.when(jnp.logical_not(left))
    def _():
        leftward.start()

    @pl.when(jnp.logical_not(last))
    def _():
        deeper.start()

    @pl.when(jnp.logical_not(first))
    def _():
        nearer.start()

    load_vel.wait()
    load_diff.wait()

    lane = lax.broadcasted_iota(jnp.int32, (ROWS, rays), 1)
    row = lax.broadcasted_iota(jnp.int32, (ROWS, rays), 0)

    def local_update(z, start):
        rows = pl.ds(start, ROWS)
        here = conc[z, pl.ds(ROWS + start, ROWS), :]
        left_cells = conc[z, pl.ds(ROWS + start - 1, ROWS), :]
        right_cells = conc[z, pl.ds(ROWS + start + 1, ROWS), :]
        lower_cells = jnp.where(lane == 0, 0.0, pltpu.roll(here, 1, 1))
        upper_cells = jnp.where(lane == rays - 1, 0.0, pltpu.roll(here, rays - 1, 1))
        spread = left_cells + right_cells + lower_cells + upper_cells
        flow = vel[1, z, rows, :] * (right_cells - left_cells) + vel[2, z, rows, :] * (
            upper_cells - lower_cells
        )
        if z > 0:
            back = conc[z - 1, pl.ds(ROWS + start, ROWS), :]
            spread = spread + back
        if z < layers - 1:
            front = conc[z + 1, pl.ds(ROWS + start, ROWS), :]
            spread = spread + front
        if 0 < z < layers - 1:
            slope = front - back
        elif z > 0:
            slope = -back
        else:
            slope = front
        flow = flow + vel[0, z, rows, :] * slope
        return here + diff[z, rows, :] * (spread - 6.0 * here) - half * flow

    def shade(mixed):
        bend = jnp.tanh(mixed)
        passed = jnp.exp((bend + 2.0) * (-1.0 / total))
        return bend, passed

    def add_cell(state, mixed):
        bend, passed = shade(mixed)
        if state is None:
            weight = 1.0 - passed
            return weight * mixed, weight * bend, weight * (mixed * mixed - 1.0), passed
        one, two, three, through = state
        weight = through * (1.0 - passed)
        return (
            one + weight * mixed,
            two + weight * bend,
            three + weight * (mixed * mixed - 1.0),
            through * passed,
        )

    order = list(range(1, groups - 1)) + [0, groups - 1]
    for g in order:
        start = g * ROWS
        edge = g in (0, groups - 1)
        state = None
        for z in range(layers):
            mixed = local_update(z, start)
            if edge or z in (0, layers - 1):
                field[z, pl.ds(start, ROWS), :] = mixed
            else:
                state = add_cell(state, mixed)
        if not edge:
            for c in range(4):
                middle[c, pl.ds(start, ROWS), :] = state[c]

    @pl.when(jnp.logical_not(first))
    def _():
        deeper.wait_recv()

    @pl.when(jnp.logical_not(last))
    def _():
        nearer.wait_recv()

    slot_of = lax.broadcasted_iota(jnp.int32, (ROWS, LANES), 1) // SLOT

    def pack(state, d):
        tile, offset = divmod(d * own, LANES)
        block = None
        for c in range(4):
            piece = state[c][:, tile * LANES : (tile + 1) * LANES]
            shift = (SLOT * c - offset) % LANES
            if shift:
                piece = pltpu.roll(piece, shift, 1)
            block = piece if block is None else jnp.where(slot_of == c, piece, block)
        return block

    def part(g, k):
        target = lax.rem(me + k, n)
        return pltpu.make_async_remote_copy(
            src_ref=send.at[g, target],
            dst_ref=recv.at[g, me],
            send_sem=part_send.at[g, k],
            recv_sem=part_recv.at[g, k],
            device_id={"depth": target},
            device_id_type=pl.DeviceIdType.MESH,
        )

    def corrected(z, start):
        rows = pl.ds(start, ROWS)
        mixed = field[z, rows, :]
        spread = diff[z, rows, :]
        if z == 0:
            mixed = mixed + z_before[rows, :] * (spread + half * vel[0, z, rows, :])
        if z == layers - 1:
            mixed = mixed + z_after[rows, :] * (spread - half * vel[0, z, rows, :])
        if start == 0:
            beside = jnp.where(row == 0, x_before[pl.ds(z, 1), :], 0.0)
            mixed = mixed + beside * (spread + half * vel[1, z, rows, :])
        if start == width - ROWS:
            beside = jnp.where(row == ROWS - 1, x_after[pl.ds(z, 1), :], 0.0)
            mixed = mixed + beside * (spread - half * vel[1, z, rows, :])
        return mixed

    waited = False
    for g in order:
        start = g * ROWS
        edge = g in (0, groups - 1)
        if edge and not waited:
            waited = True

            @pl.when(jnp.logical_not(left))
            def _():
                rightward.wait_recv()

            @pl.when(jnp.logical_not(right))
            def _():
                leftward.wait_recv()

        state = add_cell(None, corrected(0, start))
        if edge:
            for z in range(1, layers):
                state = add_cell(state, corrected(z, start))
        else:
            rows = pl.ds(start, ROWS)
            through = state[3]
            state = tuple(state[c] + through * middle[c, rows, :] for c in range(3)) + (
                through * middle[3, rows, :],
            )
            state = add_cell(state, corrected(layers - 1, start))
        state = tuple(bright * state[c] for c in range(3)) + (state[3],)
        for d in range(n):
            send[g, d] = pack(state, d)
        for k in range(1, n):
            part(g, k).start()

    for g in order:
        recv[g, me] = send[g, me]

    for g in order:
        for k in range(1, n):
            part(g, k).wait_recv()
        through = None
        for s in range(n):
            block = recv[g, s]
            passed = jnp.where(slot_of >= 2, block, pltpu.roll(block, LANES // 2, 1))
            passed = jnp.where(slot_of % 2 == 1, passed, pltpu.roll(passed, LANES - SLOT, 1))
            if through is None:
                picture, through = block, passed
            else:
                picture, through = picture + through * block, through * passed
        rows = pl.ds(g * ROWS, ROWS)
        for c in range(3):
            color = pltpu.roll(picture, LANES - SLOT * c, 1) if c else picture
            out_ref[c, rows, :] = color[:, :own]
        out_ref[3, rows, :] = (1.0 - through)[:, :own]

    @pl.when(jnp.logical_not(last))
    def _():
        deeper.wait_send()

    @pl.when(jnp.logical_not(first))
    def _():
        nearer.wait_send()

    @pl.when(jnp.logical_not(right))
    def _():
        rightward.wait_send()

    @pl.when(jnp.logical_not(left))
    def _():
        leftward.wait_send()

    for g in order:
        for k in range(1, n):
            part(g, k).wait_send()


def solution(mesh):
    n, tiles = mesh.shape["depth"], mesh.shape["tile"]

    def body(concentration, velocity, diffusivity):
        layers, width, rays = concentration.shape
        groups = width // ROWS
        own = rays // n
        assert own <= SLOT and LANES % own == 0
        scratch = [
            pltpu.VMEM((layers, width + 2 * ROWS, rays), jnp.float32),
            pltpu.VMEM(velocity.shape, jnp.float32),
            pltpu.VMEM(diffusivity.shape, jnp.float32),
            pltpu.VMEM((layers, width, rays), jnp.float32),
            pltpu.VMEM((4, width, rays), jnp.float32),
            pltpu.VMEM((width, rays), jnp.float32),
            pltpu.VMEM((width, rays), jnp.float32),
            pltpu.VMEM((2, layers, rays), jnp.float32),
            pltpu.VMEM((layers, rays), jnp.float32),
            pltpu.VMEM((layers, rays), jnp.float32),
            pltpu.VMEM((groups, n, ROWS, LANES), jnp.float32),
            pltpu.VMEM((groups, n, ROWS, LANES), jnp.float32),
            pltpu.SemaphoreType.DMA((3,)),
            pltpu.SemaphoreType.DMA((4,)),
            pltpu.SemaphoreType.DMA((4,)),
            pltpu.SemaphoreType.DMA((groups, n)),
            pltpu.SemaphoreType.DMA((groups, n)),
        ]
        return pl.pallas_call(
            functools.partial(kernel, n, tiles),
            out_shape=jax.ShapeDtypeStruct((4, width, own), jnp.float32),
            in_specs=[pl.BlockSpec(memory_space=pl.ANY)] * 3,
            out_specs=pl.BlockSpec(memory_space=pltpu.VMEM),
            scratch_shapes=scratch,
            compiler_params=pltpu.CompilerParams(collective_id=0, has_side_effects=True, vmem_limit_bytes=16 << 20),
        )(*[pltpu.with_memory_space_constraint(v, pltpu.HBM) for v in (concentration, velocity, diffusivity)])

    return jax.shard_map(
        body,
        mesh=mesh,
        in_specs=(
            P("depth", "tile", None),
            P(None, "depth", "tile", None),
            P("depth", "tile", None),
        ),
        out_specs=P(None, "tile", "depth"),
        check_vma=False,
    )
```
